256 devices in a mesh: row: 32 (over y, z), col: 8 (over x, core).
Axes of the slice: x: 4, y: 4, z: 8, core: 2. Of those that a mesh axis runs over, the one named last changes fastest.
Arguments:
- points: float32 [65536, 16], P(('row', 'col')), may hold values from -6 to 6
- inv_lengths: float32 [16], replicated, may hold values from 0.35 to 0.7
- signal_level: float32 [1], replicated, may hold values from 0.5 to 2
- noise_level: float32 [1], replicated, may hold values from 0.05 to 0.5
- right_sides: float32 [65536, 32], P(('row', 'col')), may hold values from -6 to 6
- block_counts: int32 [256], P(('row', 'col')), may hold values from 1 to 256, 49152 in all
Outputs:
- solution: float32 [65536, 32], P(('row', 'col'))
- residual: float32 [65536, 32], P(('row', 'col'))
The draws below stay inside these ranges and needn't reach their ends.
Inputs may be any that keep to these rules, and one draw needn't show every extreme that they name: `block_counts`: each block of 256 slots holds its valid points first; the slots after them are padding.
All inputs are finite; a program needn't handle non-finite values.
Results may differ from the reference program's by a relative error of at most 0.012.
The reference program's roundings to bfloat16 on the way count: a program that leaves them out, or rounds other values in their place, can miss the bound.
Values may be sent and summed in bfloat16 or wider, within the bound.
A program may use at most 64 MiB of HBM per device.

```python
import math
import jax
import jax.numpy as jnp
import numpy as np
from jax import lax

FEAT = 16
PROBES = 32
BLOCK = 256
ITERS = 2
NBLK = 256
NPTS = 65536
VALID = 49152


def draw_points(key, part):
    perm_key = jax.random.fold_in(key, 11)
    center_key = jax.random.fold_in(key, 12)
    offset_key = jax.random.fold_in(key, 13)
    groups = NPTS // 8
    shuffled = jax.random.permutation(perm_key, NPTS)
    member = shuffled // 8
    centers = 2.0 * jax.random.normal(center_key, (groups, FEAT), jnp.float32)
    offsets = 0.47 * jax.random.normal(offset_key, (NPTS, FEAT), jnp.float32)
    return jnp.clip(centers[member] + offsets, -6.0, 6.0)


def level_of(stream_key, dims, shards, least, top_value):
    loudness, own = 1.0, jax.random.fold_in(stream_key, 6)
    for dim, blocks in shards:
        heights = jnp.exp(jax.random.uniform(jax.random.fold_in(own, dim), (blocks,), jnp.float32, least / len(shards), top_value / len(shards)))
        loudness = loudness * jnp.repeat(heights, dims[dim] // blocks).reshape([-1 if axis == dim else 1 for axis in range(len(dims))])
    return loudness


def split_up(number_of, total, bound, slope):
    weights = [(1 << 20) // math.isqrt(standing ** slope) + 1 for standing in range(2, number_of + 1)]
    surplus, counts = total - bound - (number_of - 1), [1] * (number_of - 1)
    while surplus > 0:
        free = [i for i in range(number_of - 1) if counts[i] < bound]
        pool, left = sum([weights[i] for i in free]), surplus
        for i in free:
            more = min(bound - counts[i], max(1, left * weights[i] // pool), surplus)
            counts[i] = counts[i] + more
            surplus = surplus - more
    return np.array([bound] + counts)


def ragged(stream_key, number_of, total, limit, lean):
    if number_of == 2:
        one = jax.random.randint(stream_key, (), max(1, total - limit), min(limit, total - 1) + 1)
        return jnp.stack([one, total - one])
    lengths = jnp.asarray(split_up(number_of, total, limit, lean), jnp.int32)
    twos = (number_of - 1) // 2
    source_of, receiver = lengths[1:1 + 2 * twos:2], lengths[2:2 + 2 * twos:2]
    margin = jnp.minimum(source_of - 1, limit - receiver)
    passed = jax.random.randint(jax.random.fold_in(stream_key, 1), (twos,), 0, 1 << 20) % (margin + 1)
    lengths = lengths.at[1:1 + 2 * twos:2].set(source_of - passed).at[2:2 + 2 * twos:2].set(receiver + passed)
    return lengths[jax.random.permutation(jax.random.fold_in(stream_key, 2), number_of)]


def noise(key, shape, deviation, most, split=(), held_as=jnp.bfloat16):
    entries = jax.random.normal(key, shape, jnp.float32) * deviation
    if len(split) > 0:
        entries = level_of(key, shape, split, -0.22, 0.18) * entries
    return jnp.clip(entries, min=-most, max=most).astype(held_as)


def setup_inputs(seed: int = 0) -> dict:
    arg_keys = jax.random.split(jax.random.key(seed), 7)
    return {
        "points": draw_points(jax.random.fold_in(arg_keys[6], 71), 0),
        "inv_lengths": jnp.clip(jnp.exp(jax.random.uniform(arg_keys[1], (FEAT,), jnp.float32, math.log(0.35), math.log(0.7))), 0.35, 0.7),
        "signal_level": jnp.clip(jnp.exp(jax.random.uniform(arg_keys[2], (1,), jnp.float32, math.log(0.5), math.log(2.0))), 0.5, 2.0),
        "noise_level": jnp.clip(jnp.exp(jax.random.uniform(arg_keys[3], (1,), jnp.float32, math.log(0.05), math.log(0.5))), 0.05, 0.5),
        "right_sides": noise(arg_keys[4], (NPTS, PROBES), 1.0, 6.0, ((0, 256),), jnp.float32),
        "block_counts": ragged(arg_keys[5], NBLK, VALID, BLOCK, 2).astype(jnp.int32),
    }


def kernel_rows(scaled_rows, square_rows, scaled_cols, square_cols, signal):
    inner_product = lax.dot_general(scaled_rows, scaled_cols, (((1,), (1,)), ((), ())), precision=lax.Precision.HIGHEST, preferred_element_type=jnp.float32)
    distance = square_rows[:, None] + square_cols[None, :] - 2.0 * inner_product
    return (signal * jnp.exp(-0.5 * distance)).astype(jnp.bfloat16)


def reference(points, inv_lengths, signal_level, noise_level, right_sides, block_counts):
    signal = signal_level[0]
    noise_var = noise_level[0]
    scaled = points * inv_lengths[None, :]
    squares = jnp.sum(scaled * scaled, axis=1)
    slots = jnp.arange(BLOCK, dtype=jnp.int32)
    valid_rows = (slots[None, :] < block_counts[:, None]).astype(jnp.float32).reshape(NPTS, 1)
    scaled_blocks = scaled.reshape(NBLK, BLOCK, FEAT)
    square_blocks = squares.reshape(NBLK, BLOCK)

    def apply(direction):
        dir_wide = direction.astype(jnp.float32)

        def one_block(pieces):
            scaled_piece, square_piece = pieces
            kernel_block = kernel_rows(scaled_piece, square_piece, scaled, squares, signal)
            return jnp.dot(kernel_block.astype(jnp.float32), dir_wide, preferred_element_type=jnp.float32)

        products = lax.map(one_block, (scaled_blocks, square_blocks)).reshape(NPTS, PROBES)
        return valid_rows * products + noise_var * dir_wide

    residual = valid_rows * right_sides
    solution = jnp.zeros_like(residual)
    direction = residual.astype(jnp.bfloat16)
    norm_now = jnp.sum(residual * residual, axis=0)
    for iteration in range(ITERS):
        applied = apply(direction)
        dir_float = direction.astype(jnp.float32)
        curvature = jnp.sum(dir_float * applied, axis=0)
        step_size = norm_now / curvature
        solution = solution + step_size * dir_float
        residual = residual - step_size * applied
        if iteration + 1 < ITERS:
            norm_next = jnp.sum(residual * residual, axis=0)
            direction = (residual + (norm_next / norm_now) * dir_float).astype(jnp.bfloat16)
            norm_now = norm_next
    return solution, residual
```

```python
import functools

import jax
import jax.numpy as jnp
from jax import lax
from jax.experimental import pallas as pl
from jax.experimental.pallas import tpu as pltpu
from jax.sharding import PartitionSpec as P

MESH = pl.DeviceIdType.MESH
F32, BF16 = jnp.float32, jnp.bfloat16
LOG2E = 1.4426950408889634

FEAT, PROBES, BLOCK = 16, 32, 256
ZS, CORES = 8, 2
DEPTH = 128


def split3(v):
    high = v.astype(BF16).astype(F32)
    rest = v - high
    mid = rest.astype(BF16).astype(F32)
    return high, mid, rest - mid


def features(points, extra, left):
    squares = jnp.sum(points * points, axis=0, keepdims=True)
    uh, um, ul = split3(extra - 0.5 * LOG2E * squares)
    row = lax.broadcasted_iota(jnp.int32, points.shape, 0)
    base, other = (0, 3) if left else (3, 0)
    tail = jnp.where(row == base, uh, jnp.where(row == base + 1, um, jnp.where(row == base + 2, ul, 0.0)))
    tail = jnp.where((row >= other) & (row < other + 3), 1.0, tail)
    h, m, l = split3(points * LOG2E if left else points)
    parts = [h, h, m, h, l, m] if left else [h, m, h, l, h, m]
    return jnp.concatenate(parts + [tail, jnp.zeros_like(points)], axis=0)


def pack(columns):
    lane = lax.broadcasted_iota(jnp.int32, (PROBES, 128), 1)
    tile = jnp.zeros((PROBES, 128), F32)
    for i, column in enumerate(columns):
        tile = jnp.where(lane == i, column, tile)
    tile = jnp.concatenate([tile, jnp.zeros((128 - PROBES, 128), F32)], axis=0)
    return tile.T[:8, :]


def column_of(row):
    tile = jnp.concatenate([row, jnp.zeros((127, 128), F32)], axis=0)
    return tile.T[:PROBES, 0:1]


def kernel(
    ngc, ngr, xs,
    count, signal, noise, points, inv, rhs,
    sol_out, res_out,
    pts_own, r0_own, d_own, app_own, tiles,
    pts_c, pts_r, r0_c, app_c, r1_c, d_r, ybuf, rs_buf, small,
    amat, bmat, dmat, kmat,
    send, recv, pts_sem, ag_sem,
):
    row, col = lax.axis_index("row"), lax.axis_index("col")
    y, z = row // ZS, row % ZS
    x, core = col // CORES, col % CORES
    gc = z * CORES + core
    gr = y * xs + x

    def dev_c(g):
        return (y * ZS + g // CORES, x * CORES + g % CORES)

    def dev_r(g):
        return ((g // xs) * ZS + z, (g % xs) * CORES + core)

    def copy(src, dst, ss, rs, dev):
        return pltpu.make_async_remote_copy(
            src_ref=src, dst_ref=dst, send_sem=ss, recv_sem=rs, device_id=dev, device_id_type=MESH
        )

    me = (row, col)
    barrier = pltpu.get_barrier_semaphore()

    def greet(k, _):
        pl.semaphore_signal(barrier, inc=1, device_id=dev_c((gc + k) % ngc), device_id_type=MESH)
        pl.semaphore_signal(barrier, inc=1, device_id=dev_r((gr + k) % ngr), device_id_type=MESH)
        return 0

    lax.fori_loop(1, ngc, greet, 0)

    scaled = points[...] * inv[...]
    own = jnp.concatenate([scaled, jnp.zeros((BLOCK, 128 - FEAT), F32)], axis=1).T[:FEAT, :]
    slot = lax.broadcasted_iota(jnp.int32, (1, BLOCK), 1)
    valid = (slot < count[0]).astype(F32)
    rhs_t = jnp.concatenate([rhs[...], jnp.zeros((BLOCK, 128 - PROBES), F32)], axis=1).T[:PROBES, :]
    first = valid * rhs_t
    pts_own[...] = own
    pts_c[gc] = own
    pts_r[gr] = own
    r0_own[...] = first
    r0_c[gc] = first
    d_own[0] = first.astype(BF16)
    d_r[0, gr] = first.astype(BF16)
    pl.semaphore_wait(barrier, (ngc - 1) + (ngr - 1))

    def send_pts(k, _):
        copy(pts_own, pts_r.at[gr], send.at[0], recv.at[0], dev_r((gr + k) % ngr)).start()
        copy(pts_own, pts_c.at[gc], send.at[1], pts_sem.at[gc], dev_c((gc + k) % ngc)).start()
        return 0

    lax.fori_loop(1, ngc, send_pts, 0)

    def send_first(k, _):
        copy(r0_own, r0_c.at[gc], send.at[2], recv.at[2], dev_c((gc + k) % ngc)).start()
        copy(d_own.at[0], d_r.at[0, gr], send.at[3], recv.at[3], dev_r((gr + k) % ngr)).start()
        return 0

    lax.fori_loop(1, ngc, send_first, 0)

    def wait_recv(i, dst):
        copy(dst, dst, send.at[i], recv.at[i], me).wait_recv()

    def wait_send(i, src):
        copy(src, src, send.at[i], recv.at[i], me).wait_send()

    most_c, most_r = pl.ds(0, ngc - 1), pl.ds(0, ngr - 1)
    log_signal = jnp.log(jnp.full((1, BLOCK), signal[0], F32)) * LOG2E

    wait_recv(0, pts_r.at[most_r])

    def left_block(g, _):
        lanes = pl.ds(pl.multiple_of(g * BLOCK, BLOCK), BLOCK)
        amat[:, lanes] = features(pts_r[g], log_signal, True).astype(BF16)
        return 0

    lax.fori_loop(0, ngr, left_block, 0)

    def build(g):
        rows = pl.ds(pl.multiple_of(g * BLOCK, BLOCK), BLOCK)
        right = features(pts_c[g], jnp.zeros((1, BLOCK), F32), False).T.astype(BF16)
        exponent = jnp.dot(right, amat[...], preferred_element_type=F32)
        kmat[rows, :] = jnp.exp2(exponent).astype(BF16)

    def build_step(k, _):
        g = (gc + k) % ngc

        @pl.when(k > 0)
        def _():
            copy(pts_own, pts_c.at[g], send.at[1], pts_sem.at[g], me).wait_recv()

        build(g)
        return 0

    lax.fori_loop(0, ngc, build_step, 0)

    wait_recv(2, r0_c.at[most_c])

    def first_direction(g, _):
        lanes = pl.ds(pl.multiple_of(g * BLOCK, BLOCK), BLOCK)
        dmat[:, lanes] = r0_c[g].astype(BF16)
        return 0

    lax.fori_loop(0, ngc, first_direction, 0)

    def apply(it, base):
        def tile(jj, _):
            j = (gr // 2 + 1 + jj) % (ngr // 2)
            lanes = pl.ds(pl.multiple_of(j * 2 * BLOCK, 2 * BLOCK), 2 * BLOCK)
            image = jnp.dot(dmat[...], kmat[:, lanes], preferred_element_type=F32)
            for h in range(2):
                owner = 2 * j + h
                ybuf[it, owner] = image[:, h * BLOCK : (h + 1) * BLOCK]

                @pl.when(owner != gr)
                def _():
                    copy(ybuf.at[it, owner], rs_buf.at[it, gr], send.at[base], recv.at[base], dev_r(owner)).start()

            return 0

        lax.fori_loop(0, ngr // 2, tile, 0)

    def exchange(slot_index, tile, along_c):
        i = 6 + slot_index
        group, total, dev = (gc, ngc, dev_c) if along_c else (gr, ngr, dev_r)
        tiles[slot_index] = tile
        small[slot_index, group] = tile

        def go(k, _):
            copy(
                tiles.at[slot_index], small.at[slot_index, group], send.at[i], recv.at[i], dev((group + k) % total)
            ).start()
            return 0

        lax.fori_loop(1, total, go, 0)

    def gathered(slot_index, along_c):
        i = 6 + slot_index
        wait_recv(i, small.at[slot_index, most_c if along_c else most_r])
        return jnp.sum(small[slot_index], axis=0)

    def partial_curvature(it):
        def add(g, acc):
            return acc + d_r[it, g].astype(F32) * ybuf[it, g]

        acc = lax.fori_loop(0, ngr, add, jnp.zeros((PROBES, BLOCK), F32))
        return jnp.sum(acc, axis=1, keepdims=True)

    def own_image(it, base):
        wait_recv(base, rs_buf.at[it, most_r])
        rs_buf[it, gr] = ybuf[it, gr]
        return valid * jnp.sum(rs_buf[it], axis=0) + noise[0] * d_own[it].astype(F32)

    lane1 = lax.broadcasted_iota(jnp.int32, (1, 128), 1)

    def safe(v):
        return jnp.where(lane1 < PROBES, v, 1.0)

    apply(0, 4)
    wait_recv(3, d_r.at[0, most_r])
    d0 = d_own[0].astype(F32)
    exchange(
        0,
        pack([
            partial_curvature(0),
            jnp.sum(d0 * d0, axis=1, keepdims=True),
            jnp.sum(first * first, axis=1, keepdims=True),
        ]),
        True,
    )
    applied = own_image(0, 4)
    app_own[...] = applied
    app_c[gc] = applied
    partner = (row, x * CORES + 1 - core)
    hops = [1, ZS - 1, 2, ZS - 2, 3, ZS - 3, 4]
    for dz in hops:
        peer = (y * ZS + (z + dz) % ZS, col)
        copy(app_own, app_c.at[gc], send.at[11], ag_sem.at[gc], peer).start()
    copy(app_own, app_c.at[gc], send.at[11], ag_sem.at[gc], partner).start()
    exchange(1, gathered(0, True), False)
    for dz in hops:
        source = ((z + ZS - dz) % ZS) * CORES + core
        copy(app_own, app_c.at[source], send.at[11], ag_sem.at[source], me).wait_recv()
        copy(app_c.at[source], app_c.at[source], send.at[12], ag_sem.at[source], partner).start()
    totals = gathered(1, False)
    norm_now = totals[2:3]
    step_row = norm_now / safe(totals[0:1] + noise[0] * totals[1:2])
    step_one = column_of(step_row)
    for dz in [0] + hops:
        source = ((z + ZS - dz) % ZS) * CORES + 1 - core
        copy(app_own, app_c.at[source], send.at[11], ag_sem.at[source], me).wait_recv()

    def update(g, acc):
        r1 = r0_c[g] - step_one * app_c[g]
        r1_c[g] = r1
        return acc + r1 * r1

    acc = lax.fori_loop(0, ngc, update, jnp.zeros((PROBES, BLOCK), F32))
    exchange(2, pack([jnp.sum(acc, axis=1, keepdims=True)]), False)
    norm_next = gathered(2, False)[0:1]
    beta = column_of(norm_next / safe(norm_now))

    def next_direction(g, _):
        lanes = pl.ds(pl.multiple_of(g * BLOCK, BLOCK), BLOCK)
        fresh = (r1_c[g] + beta * r0_c[g].astype(BF16).astype(F32)).astype(BF16)
        dmat[:, lanes] = fresh
        return 0

    lax.fori_loop(0, ngc, next_direction, 0)
    r1_own = r1_c[gc]
    d1_bf = (r1_own + beta * d0).astype(BF16)
    d_own[1] = d1_bf
    d_r[1, gr] = d1_bf

    def send_second(k, _):
        copy(d_own.at[1], d_r.at[1, gr], send.at[13], recv.at[13], dev_r((gr + k) % ngr)).start()
        return 0

    lax.fori_loop(1, ngr, send_second, 0)

    apply(1, 5)
    wait_recv(13, d_r.at[1, most_r])
    d1 = d_own[1].astype(F32)
    exchange(3, pack([partial_curvature(1), jnp.sum(d1 * d1, axis=1, keepdims=True)]), True)
    applied = own_image(1, 5)
    exchange(4, gathered(3, True), False)
    wait_send(0, pts_r.at[most_r])
    wait_send(1, pts_c.at[most_c])
    wait_send(2, r0_c.at[most_c])
    wait_send(3, d_r.at[0, most_r])
    wait_send(4, rs_buf.at[0, most_r])
    wait_send(5, rs_buf.at[1, most_r])
    wait_send(6, small.at[0, most_c])
    wait_send(7, small.at[1, most_r])
    wait_send(8, small.at[2, most_r])
    wait_send(9, small.at[3, most_c])
    wait_send(11, app_c.at[pl.ds(0, ZS)])
    wait_send(12, app_c.at[pl.ds(0, ZS - 1)])
    wait_send(13, d_r.at[1, most_r])
    totals = gathered(4, False)
    step_two = column_of(norm_next / safe(totals[0:1] + noise[0] * totals[1:2]))
    sol_out[...] = step_one * d0 + step_two * d1
    res_out[...] = r1_own - step_two * applied
    wait_send(10, small.at[4, most_r])


def solution(mesh):
    nrow, ncol = mesh.shape["row"], mesh.shape["col"]
    xs, ys = ncol // CORES, nrow // ZS
    ngc, ngr = ZS * CORES, xs * ys

    def body(points, inv_lengths, signal_level, noise_level, right_sides, block_counts):
        vmem, smem = pl.BlockSpec(memory_space=pltpu.VMEM), pl.BlockSpec(memory_space=pltpu.SMEM)
        block = jax.ShapeDtypeStruct((PROBES, BLOCK), F32)
        sol, res = pl.pallas_call(
            functools.partial(kernel, ngc, ngr, xs),
            out_shape=(block, block),
            in_specs=[smem, smem, smem, vmem, vmem, vmem],
            out_specs=(vmem, vmem),
            scratch_shapes=[
                pltpu.VMEM((FEAT, BLOCK), F32),
                pltpu.VMEM((PROBES, BLOCK), F32),
                pltpu.VMEM((2, PROBES, BLOCK), BF16),
                pltpu.VMEM((PROBES, BLOCK), F32),
                pltpu.VMEM((5, 8, 128), F32),
                pltpu.VMEM((ngc, FEAT, BLOCK), F32),
                pltpu.VMEM((ngr, FEAT, BLOCK), F32),
                pltpu.VMEM((ngc, PROBES, BLOCK), F32),
                pltpu.VMEM((ngc, PROBES, BLOCK), F32),
                pltpu.VMEM((ngc, PROBES, BLOCK), F32),
                pltpu.VMEM((2, ngr, PROBES, BLOCK), BF16),
                pltpu.VMEM((2, ngr, PROBES, BLOCK), F32),
                pltpu.VMEM((2, ngr, PROBES, BLOCK), F32),
                pltpu.VMEM((5, 16, 8, 128), F32),
                pltpu.VMEM((DEPTH, ngr * BLOCK), BF16),
                pltpu.VMEM((8, 128), BF16),
                pltpu.VMEM((PROBES, ngc * BLOCK), BF16),
                pltpu.VMEM((ngc * BLOCK, ngr * BLOCK), BF16),
                pltpu.SemaphoreType.DMA((14,)),
                pltpu.SemaphoreType.DMA((14,)),
                pltpu.SemaphoreType.DMA((ngc,)),
                pltpu.SemaphoreType.DMA((ngc,)),
            ],
            compiler_params=pltpu.CompilerParams(
                collective_id=0, has_side_effects=True, vmem_limit_bytes=60 * 1024 * 1024
            ),
            name="cg",
        )(block_counts, signal_level, noise_level, points, inv_lengths.reshape(1, FEAT), right_sides)
        return sol.T, res.T

    in_specs = (P(("row", "col"), None), P(), P(), P(), P(("row", "col"), None), P(("row", "col")))
    out_specs = (P(("row", "col"), None), P(("row", "col"), None))
    return jax.shard_map(body, mesh=mesh, in_specs=in_specs, out_specs=out_specs, check_vma=False)
```

```python
import functools

import jax
import jax.numpy as jnp
from jax import lax
from jax.experimental import pallas as pl
from jax.experimental.pallas import tpu as pltpu
from jax.sharding import PartitionSpec as P

MESH = pl.DeviceIdType.MESH
F32, BF16 = jnp.float32, jnp.bfloat16
LOG2E = 1.4426950408889634

FEAT, PROBES, BLOCK = 16, 32, 256
ZS, CORES = 8, 2
DEPTH = 128


def split3(v):
    high = v.astype(BF16).astype(F32)
    rest = v - high
    mid = rest.astype(BF16).astype(F32)
    return high, mid, rest - mid


def features(points, extra, left):
    squares = jnp.sum(points * points, axis=0, keepdims=True)
    uh, um, ul = split3(extra - 0.5 * LOG2E * squares)
    row = lax.broadcasted_iota(jnp.int32, points.shape, 0)
    base, other = (0, 3) if left else (3, 0)
    tail = jnp.where(row == base, uh, jnp.where(row == base + 1, um, jnp.where(row == base + 2, ul, 0.0)))
    tail = jnp.where((row >= other) & (row < other + 3), 1.0, tail)
    h, m, l = split3(points * LOG2E if left else points)
    parts = [h, h, m, h, l, m] if left else [h, m, h, l, h, m]
    return jnp.concatenate(parts + [tail, jnp.zeros_like(points)], axis=0)


def pack(columns):
    rest = [jnp.zeros((PROBES, 1), F32)] * (128 // PROBES - len(columns))
    column = jnp.concatenate(list(columns) + rest, axis=0)
    return jnp.broadcast_to(column, (128, 128)).T[0:1, :]


def unpack(row, count):
    column = jnp.broadcast_to(row, (128, 128)).T[:, 0:1]
    return [column[i * PROBES : (i + 1) * PROBES] for i in range(count)]


def kernel(
    ngc, ngr, xs,
    count, signal, noise, points_hbm, inv_hbm, rhs_hbm,
    out,
    points, inv, rhs, load, pts_own, r0_own, d_own, app_own, tiles,
    pts_c, pts_r, d0_c, r0_c, app_c, d_r, ybuf, rs_buf, small,
    amat, bmat, dmat, kmat,
    send, recv, relay, pts_sem, d0_sem, r0_sem, ag_sem,
):
    row, col = lax.axis_index("row"), lax.axis_index("col")
    y, z = lax.div(row, ZS), lax.rem(row, ZS)
    x, core = lax.div(col, CORES), lax.rem(col, CORES)
    gc = z * CORES + core
    gr = y * xs + x
    me = (row, col)
    partner = (row, x * CORES + 1 - core)
    tile_count = ngr // 2

    def around(g, k, total):
        return lax.rem(g + k, total)

    def dev_c(g):
        return (y * ZS + lax.div(g, CORES), x * CORES + lax.rem(g, CORES))

    def dev_r(g):
        return (lax.div(g, xs) * ZS + z, lax.rem(g, xs) * CORES + core)

    peers_c = [dev_c(around(gc, k, ngc)) for k in range(1, ngc)]
    peers_r = [dev_r(around(gr, k, ngr)) for k in range(1, ngr)]

    def at_z(dz, c=core):
        return around(z, dz % ZS, ZS) * CORES + c

    def chip_z(dz):
        return (y * ZS + around(z, dz % ZS, ZS), col)

    sources = [at_z(-dz) for dz in (1, -1, 2, -2, 3, -3, 4)]
    others = [at_z(-dz, 1 - core) for dz in (0, 1, -1, 2, -2, 3, -3, 4)]
    far_source = around(z, 6 - 4 * core, ZS) * CORES + core
    far_target = (y * ZS + around(z, 2 + 4 * core, ZS), col)

    def copy(src, dst, ss, rs, dev):
        return pltpu.make_async_remote_copy(
            src_ref=src, dst_ref=dst, send_sem=ss, recv_sem=rs, device_id=dev, device_id_type=MESH
        )

    def wait_recv(i, dst):
        copy(dst, dst, send.at[i], recv.at[i], me).wait_recv()

    def wait_send(i, src):
        copy(src, src, send.at[i], recv.at[i], me).wait_send()

    most_c, most_r = pl.ds(0, ngc - 1), pl.ds(0, ngr - 1)

    def spread(i, block, slots, sems):
        for dz in (1, -1, 2, -2):
            copy(block, slots.at[gc], send.at[i], sems.at[gc], chip_z(dz)).start()
        copy(block, slots.at[gc], send.at[i], sems.at[gc], partner).start()

    def arrived(slots, sems, g):
        copy(slots.at[g], slots.at[g], send.at[0], sems.at[g], me).wait_recv()

    def hand_on(j, slots, sems, g, dev):
        copy(slots.at[g], slots.at[g], relay.at[j], sems.at[g], dev).start()

    def near(j, slots, sems, use=None):
        for dz in (1, -1, 2, -2):
            g = at_z(-dz)
            arrived(slots, sems, g)
            if dz == 2 or dz == -2:
                hand_on(j, slots, sems, g, chip_z(dz // 2))
            if dz == -2:
                hand_on(j, slots, sems, far_source, far_target)
            hand_on(j, slots, sems, g, partner)
            if use is not None:
                use(g)

    def far(j, slots, sems, use=None):
        for dz in (3, -3, 4):
            g = at_z(-dz)
            arrived(slots, sems, g)
            hand_on(j, slots, sems, g, partner)
            if use is not None:
                use(g)

    def drain(i, j, slots):
        copy(slots.at[pl.ds(0, 5)], slots.at[pl.ds(0, 5)], send.at[i], recv.at[0], me).wait_send()
        copy(slots.at[pl.ds(0, 10)], slots.at[pl.ds(0, 10)], relay.at[j], recv.at[0], me).wait_send()

    loads = [
        pltpu.make_async_copy(source, target, load.at[i])
        for i, (source, target) in enumerate([(points_hbm, points), (inv_hbm, inv), (rhs_hbm, rhs)])
    ]
    for one in loads:
        one.start()
    barrier = pltpu.get_barrier_semaphore()
    for peer in peers_c + peers_r:
        pl.semaphore_signal(barrier, inc=1, device_id=peer, device_id_type=MESH)

    for one in loads:
        one.wait()
    inv_row = jnp.concatenate([inv[...], jnp.zeros((1, 128 - FEAT), F32)], axis=1)
    inv_column = jnp.broadcast_to(inv_row, (128, 128)).T[:FEAT, 0:1]
    own = points[...] * inv_column
    slot = lax.broadcasted_iota(jnp.int32, (1, BLOCK), 1)
    valid = (slot < count[0]).astype(F32)
    first = valid * rhs[...]
    first_bf = first.astype(BF16)
    pts_own[...] = own
    pts_c[gc] = own
    pts_r[gr] = own
    r0_own[...] = first
    r0_c[gc] = first
    d_own[0] = first_bf
    d0_c[gc] = first_bf
    d_r[0, gr] = first_bf
    pl.semaphore_wait(barrier, (ngc - 1) + (ngr - 1))

    spread(1, pts_own, pts_c, pts_sem)
    for peer in peers_r:
        copy(pts_own, pts_r.at[gr], send.at[0], recv.at[0], peer).start()
    spread(2, d_own.at[0], d0_c, d0_sem)
    for peer in peers_r:
        copy(d_own.at[0], d_r.at[0, gr], send.at[3], recv.at[3], peer).start()
    spread(14, r0_own, r0_c, r0_sem)

    log_signal = jnp.log(jnp.full((1, BLOCK), signal[0], F32)) * LOG2E

    def lanes_of(g, width=1):
        return pl.ds(pl.multiple_of(g * width * BLOCK, width * BLOCK), width * BLOCK)

    def right_block(g):
        right = features(pts_c[g], jnp.zeros((1, BLOCK), F32), False).T.astype(BF16)
        bmat[lanes_of(g), :] = right

    right_block(gc)
    near(0, pts_c, pts_sem, right_block)
    near(1, d0_c, d0_sem)
    far(0, pts_c, pts_sem, right_block)
    for g in others:
        arrived(pts_c, pts_sem, g)
        right_block(g)
    wait_recv(0, pts_r.at[most_r])

    def left_block(g, _):
        amat[:, lanes_of(g)] = features(pts_r[g], log_signal, True).astype(BF16)
        return 0

    lax.fori_loop(0, ngr, left_block, 0)

    def tile_at(k):
        return around(lax.div(gr, 2), k, tile_count)

    def build(k):
        lanes = lanes_of(tile_at(k), 2)
        exponent = jnp.dot(bmat[...], amat[:, lanes], preferred_element_type=F32)
        values = jnp.exp2(exponent).astype(BF16)
        kmat[:, lanes] = values
        return values

    def image_of(it, k, values=None):
        j = tile_at(k)
        if values is None:
            values = kmat[:, lanes_of(j, 2)]
        image = jnp.dot(dmat[...], values, preferred_element_type=F32)
        for h in range(2):
            ybuf[it, 2 * j + h] = image[:, h * BLOCK : (h + 1) * BLOCK]
        return j

    def send_image(it, owner):
        i = 4 + it
        copy(ybuf.at[it, owner], rs_buf.at[it, gr], send.at[i], recv.at[i], dev_r(owner)).start()

    def finish_own(it):
        image_of(it, 0)
        send_image(it, 2 * lax.div(gr, 2) + 1 - lax.rem(gr, 2))

    early = 2

    def build_only(k, _):
        build(k)
        return 0

    lax.fori_loop(0, early, build_only, 0)

    far(1, d0_c, d0_sem)
    near(2, r0_c, r0_sem)
    for g in others:
        arrived(d0_c, d0_sem, g)
    for g in range(ngc):
        dmat[:, g * BLOCK : (g + 1) * BLOCK] = d0_c[g]

    def build_and_apply(k, _):
        j = image_of(0, k, build(k))
        send_image(0, 2 * j)
        send_image(0, 2 * j + 1)
        return 0

    lax.fori_loop(early, tile_count, build_and_apply, 0)
    far(2, r0_c, r0_sem)

    def apply_only(k, _):
        j = image_of(0, k)
        send_image(0, 2 * j)
        send_image(0, 2 * j + 1)
        return 0

    lax.fori_loop(1, early, apply_only, 0)
    finish_own(0)

    def exchange(s, message, along_c):
        i = 6 + s
        group, devices = (gc, peers_c) if along_c else (gr, peers_r)
        tiles[s] = message
        small[s, group] = message
        for device in devices:
            copy(tiles.at[s], small.at[s, group], send.at[i], recv.at[i], device).start()

    def gathered(s, along_c):
        wait_recv(6 + s, small.at[s, most_c if along_c else most_r])
        return jnp.sum(small[s], axis=0)

    def sum_of(v):
        return jnp.sum(v, axis=1, keepdims=True)

    def curvature_part(it):
        acc = jnp.zeros((PROBES, BLOCK), F32)
        for g in range(ngr):
            acc = acc + d_r[it, g].astype(F32) * ybuf[it, g]
        own_direction = d_own[it].astype(F32)
        return sum_of(acc) + noise[0] * sum_of(own_direction * own_direction)

    def own_image(it):
        wait_recv(4 + it, rs_buf.at[it, most_r])
        rs_buf[it, gr] = ybuf[it, gr]
        return valid * jnp.sum(rs_buf[it], axis=0) + noise[0] * d_own[it].astype(F32)

    def lane_roll(v, shift):
        return pltpu.roll(v, shift % 128, v.ndim - 1)

    def joined(s, along_c):
        wait_recv(6 + s, small.at[s, most_c if along_c else most_r])
        part = small[s]
        weight, vertex, least = [lane_roll(part, -32 * i) for i in (1, 2, 3)]
        weights = jnp.sum(weight, axis=0)
        middle = jnp.where(weights > 0.0, jnp.sum(weight * vertex, axis=0) / weights, 0.0)
        away = vertex - middle[None]
        return jnp.sum(part, axis=0), weights, middle, jnp.sum(least + weight * away * away, axis=0)

    lane = lax.broadcasted_iota(jnp.int32, (1, 128), 1)

    def side_by_side(rows):
        out_row = rows[0]
        for i, one in enumerate(rows[1:], 1):
            out_row = jnp.where(lane >= PROBES * i, lane_roll(one, PROBES * i), out_row)
        return out_row

    wait_recv(3, d_r.at[0, most_r])
    applied = own_image(0)
    app_own[...] = applied
    app_c[gc] = applied
    spread(11, app_own, app_c, ag_sem)
    weight = sum_of(applied * applied)
    vertex = jnp.where(weight > 0.0, sum_of(first * applied) / weight, 0.0)
    off = first - vertex * applied
    exchange(0, pack([curvature_part(0), weight, vertex, sum_of(off * off)]), True)
    near(3, app_c, ag_sem)
    exchange(1, side_by_side(joined(0, True)), False)
    for g in others:
        arrived(r0_c, r0_sem, g)
    far(3, app_c, ag_sem)
    curvature, weight, vertex, least = joined(1, False)
    norm_now = least + weight * vertex * vertex
    step_row = norm_now / curvature
    norm_next = least + weight * (step_row - vertex) * (step_row - vertex)
    step_one, beta, norm_next = unpack(side_by_side([step_row, norm_next / norm_now, norm_next]), 3)
    for g in others:
        arrived(app_c, ag_sem, g)
    for g in range(ngc):
        r1 = r0_c[g] - step_one * app_c[g]
        dmat[:, g * BLOCK : (g + 1) * BLOCK] = (r1 + beta * d0_c[g].astype(F32)).astype(BF16)
    d0 = d_own[0].astype(F32)
    r1_own = first - step_one * applied
    d1_bf = (r1_own + beta * d0).astype(BF16)
    d_own[1] = d1_bf
    d_r[1, gr] = d1_bf
    for peer in peers_r:
        copy(d_own.at[1], d_r.at[1, gr], send.at[13], recv.at[13], peer).start()

    def second_apply(k, _):
        j = image_of(1, k)
        send_image(1, 2 * j)
        send_image(1, 2 * j + 1)
        return 0

    lax.fori_loop(1, tile_count, second_apply, 0)
    finish_own(1)
    wait_recv(13, d_r.at[1, most_r])
    exchange(2, pack([curvature_part(1)]), True)
    drain(1, 0, pts_c)
    drain(2, 1, d0_c)
    drain(14, 2, r0_c)
    drain(11, 3, app_c)
    wait_send(0, pts_r.at[most_r])
    wait_send(3, d_r.at[0, most_r])
    wait_send(4, rs_buf.at[0, most_r])
    wait_send(6, small.at[0, most_c])
    wait_send(7, small.at[1, most_r])
    wait_send(13, d_r.at[1, most_r])
    exchange(3, gathered(2, True), False)
    applied = own_image(1)
    wait_send(5, rs_buf.at[1, most_r])
    wait_send(8, small.at[2, most_c])
    (curvature,) = unpack(gathered(3, False), 1)
    step_two = norm_next / curvature
    out[:PROBES, :] = step_one * d0 + step_two * d1_bf.astype(F32)
    out[PROBES:, :] = r1_own - step_two * applied
    wait_send(9, small.at[3, most_r])


def solution(mesh):
    nrow, ncol = mesh.shape["row"], mesh.shape["col"]
    xs, ys = ncol // CORES, nrow // ZS
    ngc, ngr = ZS * CORES, xs * ys

    def body(points, inv_lengths, signal_level, noise_level, right_sides, block_counts):
        vmem, smem = pl.BlockSpec(memory_space=pltpu.VMEM), pl.BlockSpec(memory_space=pltpu.SMEM)
        anywhere = pl.BlockSpec(memory_space=pl.ANY)
        result = pl.pallas_call(
            functools.partial(kernel, ngc, ngr, xs),
            out_shape=jax.ShapeDtypeStruct((2 * PROBES, BLOCK), F32),
            in_specs=[smem, smem, smem, anywhere, anywhere, anywhere],
            out_specs=vmem,
            scratch_shapes=[
                pltpu.VMEM((FEAT, BLOCK), F32),
                pltpu.VMEM((1, FEAT), F32),
                pltpu.VMEM((PROBES, BLOCK), F32),
                pltpu.SemaphoreType.DMA((3,)),
                pltpu.VMEM((FEAT, BLOCK), F32),
                pltpu.VMEM((PROBES, BLOCK), F32),
                pltpu.VMEM((2, PROBES, BLOCK), BF16),
                pltpu.VMEM((PROBES, BLOCK), F32),
                pltpu.VMEM((4, 1, 128), F32),
                pltpu.VMEM((ngc, FEAT, BLOCK), F32),
                pltpu.VMEM((ngr, FEAT, BLOCK), F32),
                pltpu.VMEM((ngc, PROBES, BLOCK), BF16),
                pltpu.VMEM((ngc, PROBES, BLOCK), F32),
                pltpu.VMEM((ngc, PROBES, BLOCK), F32),
                pltpu.VMEM((2, ngr, PROBES, BLOCK), BF16),
                pltpu.VMEM((2, ngr, PROBES, BLOCK), F32),
                pltpu.VMEM((2, ngr, PROBES, BLOCK), F32),
                pltpu.VMEM((4, ngc, 1, 128), F32),
                pltpu.VMEM((DEPTH, ngr * BLOCK), BF16),
                pltpu.VMEM((ngc * BLOCK, DEPTH), BF16),
                pltpu.VMEM((PROBES, ngc * BLOCK), BF16),
                pltpu.VMEM((ngc * BLOCK, ngr * BLOCK), BF16),
                pltpu.SemaphoreType.DMA((15,)),
                pltpu.SemaphoreType.DMA((14,)),
                pltpu.SemaphoreType.DMA((4,)),
                pltpu.SemaphoreType.DMA((ngc,)),
                pltpu.SemaphoreType.DMA((ngc,)),
                pltpu.SemaphoreType.DMA((ngc,)),
                pltpu.SemaphoreType.DMA((ngc,)),
            ],
            compiler_params=pltpu.CompilerParams(
                collective_id=0, has_side_effects=True, vmem_limit_bytes=60 * 1024 * 1024
            ),
            name="cg",
        )(block_counts, signal_level, noise_level, points.T, inv_lengths.reshape(1, FEAT), right_sides.T)
        return result[:PROBES].T, result[PROBES:].T

    in_specs = (P(("row", "col"), None), P(), P(), P(), P(("row", "col"), None), P(("row", "col")))
    out_specs = (P(("row", "col"), None), P(("row", "col"), None))
    return jax.shard_map(body, mesh=mesh, in_specs=in_specs, out_specs=out_specs, check_vma=False)
```

```python
import functools

import jax
import jax.numpy as jnp
from jax import lax
from jax.experimental import pallas as pl
from jax.experimental.pallas import tpu as pltpu
from jax.sharding import PartitionSpec as P

MESH = pl.DeviceIdType.MESH
F32, BF16 = jnp.float32, jnp.bfloat16
LOG2E = 1.4426950408889634

FEAT, PROBES, BLOCK = 16, 32, 256
ZS, CORES = 8, 2
DEPTH = 128


def split3(v):
    high = v.astype(BF16).astype(F32)
    rest = v - high
    mid = rest.astype(BF16).astype(F32)
    return high, mid, rest - mid


def features(points, extra, left):
    squares = jnp.sum(points * points, axis=0, keepdims=True)
    uh, um, ul = split3(extra - 0.5 * LOG2E * squares)
    row = lax.broadcasted_iota(jnp.int32, points.shape, 0)
    base, other = (0, 3) if left else (3, 0)
    tail = jnp.where(row == base, uh, jnp.where(row == base + 1, um, jnp.where(row == base + 2, ul, 0.0)))
    tail = jnp.where((row >= other) & (row < other + 3), 1.0, tail)
    h, m, l = split3(points * LOG2E if left else points)
    parts = [h, h, m, h, l, m] if left else [h, m, h, l, h, m]
    return jnp.concatenate(parts + [tail, jnp.zeros_like(points)], axis=0)


def pack(columns):
    rest = [jnp.zeros((PROBES, 1), F32)] * (128 // PROBES - len(columns))
    column = jnp.concatenate(list(columns) + rest, axis=0)
    return jnp.broadcast_to(column, (128, 128)).T[0:1, :]


def unpack(row, count):
    column = jnp.broadcast_to(row, (128, 128)).T[:, 0:1]
    return [column[i * PROBES : (i + 1) * PROBES] for i in range(count)]


def kernel(
    ngc, ngr, xs,
    count, signal, noise, points_hbm, inv_hbm, rhs_hbm,
    out,
    points, inv, rhs, load, pts_own, r0_own, d0_own, d1_own, app_own, tiles,
    pts_c, pts_r, d0_c, r0_c, app_c, d1_r, ybuf, rs_buf, small,
    amat, bmat, dmat, kmat,
    send, recv, relay, pts_sem, left_sem, d0_sem, r0_sem, ag_sem,
):
    row, col = lax.axis_index("row"), lax.axis_index("col")
    y, z = lax.div(row, ZS), lax.rem(row, ZS)
    x, core = lax.div(col, CORES), lax.rem(col, CORES)
    gc = z * CORES + core
    gr = y * xs + x
    me = (row, col)
    partner = (row, x * CORES + 1 - core)
    pairs = ngr // 2
    half = ngc * BLOCK // 2

    def around(g, k, total):
        return lax.rem(g + k, total)

    def dev_c(g):
        return (y * ZS + lax.div(g, CORES), x * CORES + lax.rem(g, CORES))

    def dev_r(g):
        return (lax.div(g, xs) * ZS + z, lax.rem(g, xs) * CORES + core)

    def at_z(dz, c=core):
        return around(z, dz % ZS, ZS) * CORES + c

    def chip_z(dz):
        return (y * ZS + around(z, dz % ZS, ZS), col)

    def pair_at(k):
        return around(lax.div(gr, 2), k, pairs)

    peers_c = [dev_c(around(gc, k, ngc)) for k in range(1, ngc)]
    peers_r = [dev_r(2 * lax.div(gr, 2) + 1 - lax.rem(gr, 2))]
    for k in range(1, pairs):
        peers_r += [dev_r(2 * pair_at(pairs - k) + h) for h in range(2)]
    first_hops, later_hops = [1, -1, 2], [-2, 3, -3, 4]
    hops = first_hops + later_hops
    places = [(dz, side) for dz in [0] + hops for side in range(2)]
    order = [at_z(-dz, 1 - core if side else core) for dz, side in places]
    others = order[1::2]
    far_source = around(z, 6 - 4 * core, ZS) * CORES + core
    far_target = (y * ZS + around(z, 2 + 4 * core, ZS), col)

    def copy(src, dst, ss, rs, dev):
        return pltpu.make_async_remote_copy(
            src_ref=src, dst_ref=dst, send_sem=ss, recv_sem=rs, device_id=dev, device_id_type=MESH
        )

    def wait_recv(i, dst):
        copy(dst, dst, send.at[i], recv.at[i], me).wait_recv()

    def wait_send(i, src):
        copy(src, src, send.at[i], recv.at[0], me).wait_send()

    most_c, most_r = pl.ds(0, ngc - 1), pl.ds(0, ngr - 1)

    def spread(i, block, slots, sems, targets):
        copy(block, slots.at[gc], send.at[i], sems.at[gc], partner).start()
        for dz in targets:
            copy(block, slots.at[gc], send.at[i], sems.at[gc], chip_z(dz)).start()

    def arrived(slots, sems, g):
        copy(slots.at[g], slots.at[g], send.at[0], sems.at[g], me).wait_recv()

    def hand_on(j, slots, sems, g, dev):
        copy(slots.at[g], slots.at[g], relay.at[j], sems.at[g], dev).start()

    def pass_over(j, slots, sems, distances):
        for dz in distances:
            arrived(slots, sems, at_z(-dz))
            hand_on(j, slots, sems, at_z(-dz), partner)

    def drain(i, j, slots, sent, handed):
        copy(slots.at[pl.ds(0, sent)], slots.at[pl.ds(0, sent)], send.at[i], recv.at[0], me).wait_send()
        copy(slots.at[pl.ds(0, handed)], slots.at[pl.ds(0, handed)], relay.at[j], recv.at[0], me).wait_send()

    loads = [
        pltpu.make_async_copy(source, target, load.at[i])
        for i, (source, target) in enumerate([(points_hbm, points), (inv_hbm, inv), (rhs_hbm, rhs)])
    ]
    for one in loads:
        one.start()
    barrier = pltpu.get_barrier_semaphore()
    for peer in peers_c + peers_r:
        pl.semaphore_signal(barrier, inc=1, device_id=peer, device_id_type=MESH)

    for one in loads:
        one.wait()
    inv_row = jnp.concatenate([inv[...], jnp.zeros((1, 128 - FEAT), F32)], axis=1)
    inv_column = jnp.broadcast_to(inv_row, (128, 128)).T[:FEAT, 0:1]
    own = points[...] * inv_column
    slot = lax.broadcasted_iota(jnp.int32, (1, BLOCK), 1)
    valid = (slot < count[0]).astype(F32)
    first = valid * rhs[...]
    first_bf = first.astype(BF16)
    d0 = first_bf.astype(F32)
    pts_own[...] = own
    pts_c[gc] = own
    pts_r[gr] = own
    r0_own[...] = first
    r0_c[gc] = first
    d0_own[...] = first_bf
    d0_c[gc] = first_bf
    pl.semaphore_wait(barrier, (ngc - 1) + (ngr - 1))

    spread(1, pts_own, pts_c, pts_sem, hops)
    for peer in peers_r:
        copy(pts_own, pts_r.at[gr], send.at[0], left_sem.at[gr], peer).start()
    spread(2, d0_own, d0_c, d0_sem, hops)
    spread(3, r0_own, r0_c, r0_sem, hops)

    log_signal = jnp.log(jnp.full((1, BLOCK), signal[0], F32)) * LOG2E

    def lanes_of(g, width=1):
        return pl.ds(pl.multiple_of(g * width * BLOCK, width * BLOCK), width * BLOCK)

    def right_block(i):
        right = features(pts_c[order[i]], jnp.zeros((1, BLOCK), F32), False).T.astype(BF16)
        bmat[i * BLOCK : (i + 1) * BLOCK, :] = right

    def left_block(g):
        amat[:, lanes_of(g)] = features(pts_r[g], log_signal, True).astype(BF16)

    right_block(0)
    left_block(gr)
    pass_over(0, pts_c, pts_sem, first_hops)
    for i in range(2, ngc // 2, 2):
        right_block(i)
    for i in range(1, ngc // 2, 2):
        arrived(pts_c, pts_sem, order[i])
        right_block(i)
    pass_over(0, pts_c, pts_sem, later_hops)

    def build(start, lanes):
        exponent = jnp.dot(bmat[start : start + half, :], amat[:, lanes], preferred_element_type=F32)
        values = jnp.exp2(exponent).astype(BF16)
        kmat[start : start + half, lanes] = values
        return values

    def near_part(k, _):
        j = pair_at(k)
        for h in range(2):

            @pl.when(2 * j + h != gr)
            def _():
                arrived(pts_r, left_sem, 2 * j + h)
                left_block(2 * j + h)

        build(0, lanes_of(j, 2))
        return 0

    lax.fori_loop(0, pairs - 3, near_part, 0)
    pass_over(1, d0_c, d0_sem, hops)
    lax.fori_loop(pairs - 3, pairs, near_part, 0)
    for i in range(ngc // 2, ngc, 2):
        right_block(i)
    for i in range(ngc // 2 + 1, ngc, 2):
        arrived(pts_c, pts_sem, order[i])
        right_block(i)
    for g in others:
        arrived(d0_c, d0_sem, g)
    for i, g in enumerate(order):
        dmat[:, i * BLOCK : (i + 1) * BLOCK] = d0_c[g]

    def send_image(it, j, image):
        for h in range(2):
            owner = 2 * j + h
            ybuf[it, owner] = image[:, h * BLOCK : (h + 1) * BLOCK]

            @pl.when(owner != gr)
            def _():
                copy(ybuf.at[it, owner], rs_buf.at[it, gr], send.at[4 + it], recv.at[4 + it], dev_r(owner)).start()

    def far_part(k, _):
        j = pair_at(k)
        lanes = lanes_of(j, 2)
        image = jnp.dot(dmat[:, :half], kmat[:half, lanes], preferred_element_type=F32)
        image = image + jnp.dot(dmat[:, half:], build(half, lanes), preferred_element_type=F32)
        send_image(0, j, image)
        return 0

    lax.fori_loop(1, pairs + 1, far_part, 0)
    pass_over(2, r0_c, r0_sem, hops)

    def sum_of(v):
        return jnp.sum(v, axis=1, keepdims=True)

    def own_image(it, direction):
        wait_recv(4 + it, rs_buf.at[it, most_r])
        rs_buf[it, gr] = ybuf[it, gr]
        return valid * jnp.sum(rs_buf[it], axis=0) + noise[0] * direction

    def exchange(s, message, along_c):
        i = 6 + s
        group, devices = (gc, peers_c) if along_c else (gr, peers_r)
        tiles[s] = message
        small[s, group] = message
        for device in devices:
            copy(tiles.at[s], small.at[s, group], send.at[i], recv.at[i], device).start()

    def gathered(s, along_c):
        wait_recv(6 + s, small.at[s, most_c if along_c else most_r])
        return small[s]

    def lane_roll(v, shift):
        return pltpu.roll(v, shift % 128, v.ndim - 1)

    def joined(part):
        weight, vertex, least = [lane_roll(part, -PROBES * i) for i in (1, 2, 3)]
        weights = jnp.sum(weight, axis=0)
        middle = jnp.where(weights > 0.0, jnp.sum(weight * vertex, axis=0) / weights, 0.0)
        away = vertex - middle[None]
        return jnp.sum(part, axis=0), weights, middle, jnp.sum(least + weight * away * away, axis=0)

    lane = lax.broadcasted_iota(jnp.int32, (1, 128), 1)

    def side_by_side(rows):
        result = rows[0]
        for i, one in enumerate(rows[1:], 1):
            result = jnp.where(lane >= PROBES * i, lane_roll(one, PROBES * i), result)
        return result

    applied = own_image(0, d0)
    app_own[...] = applied
    app_c[gc] = applied
    spread(11, app_own, app_c, ag_sem, (1, -1, 2, -2))
    weight = sum_of(applied * applied)
    vertex = jnp.where(weight > 0.0, sum_of(first * applied) / weight, 0.0)
    off = first - vertex * applied
    exchange(0, pack([sum_of(d0 * applied), weight, vertex, sum_of(off * off)]), False)
    for dz in (1, -1, 2, -2):
        g = at_z(-dz)
        arrived(app_c, ag_sem, g)
        if dz == 2 or dz == -2:
            hand_on(3, app_c, ag_sem, g, chip_z(dz // 2))
        if dz == -2:
            hand_on(3, app_c, ag_sem, far_source, far_target)
        hand_on(3, app_c, ag_sem, g, partner)
    exchange(1, side_by_side(joined(gathered(0, False))), True)
    pass_over(3, app_c, ag_sem, (3, -3, 4))
    curvature, weight, vertex, least = joined(gathered(1, True))
    norm_now = least + weight * vertex * vertex
    step_row = norm_now / curvature
    norm_next = least + weight * (step_row - vertex) * (step_row - vertex)
    step_one, beta, norm_next = unpack(side_by_side([step_row, norm_next / norm_now, norm_next]), 3)
    for g in others:
        arrived(r0_c, r0_sem, g)
    for g in others:
        arrived(app_c, ag_sem, g)
    for i, g in enumerate(order):
        r1 = r0_c[g] - step_one * app_c[g]
        dmat[:, i * BLOCK : (i + 1) * BLOCK] = (r1 + beta * d0_c[g].astype(F32)).astype(BF16)
    r1_own = first - step_one * applied
    d1_bf = (r1_own + beta * d0).astype(BF16)
    d1 = d1_bf.astype(F32)
    d1_own[...] = d1_bf
    d1_r[gr] = d1_bf
    for peer in peers_r:
        copy(d1_own, d1_r.at[gr], send.at[10], recv.at[10], peer).start()

    def second_part(k, _):
        j = pair_at(k)
        send_image(1, j, jnp.dot(dmat[...], kmat[:, lanes_of(j, 2)], preferred_element_type=F32))
        return 0

    lax.fori_loop(1, pairs + 1, second_part, 0)
    wait_recv(10, d1_r.at[most_r])
    acc = jnp.zeros((PROBES, BLOCK), F32)
    for g in range(ngr):
        acc = acc + d1_r[g].astype(F32) * ybuf[1, g]
    exchange(2, pack([sum_of(acc) + noise[0] * sum_of(d1 * d1)]), True)
    drain(1, 0, pts_c, ZS, ZS - 1)
    drain(2, 1, d0_c, ZS, ZS - 1)
    drain(3, 2, r0_c, ZS, ZS - 1)
    drain(11, 3, app_c, 5, 10)
    wait_send(0, pts_r.at[most_r])
    wait_send(4, rs_buf.at[0, most_r])
    wait_send(6, small.at[0, most_r])
    wait_send(7, small.at[1, most_c])
    exchange(3, jnp.sum(gathered(2, True), axis=0), False)
    wait_send(8, small.at[2, most_c])
    wait_send(10, d1_r.at[most_r])
    applied = own_image(1, d1)
    wait_send(5, rs_buf.at[1, most_r])
    (curvature,) = unpack(jnp.sum(gathered(3, False), axis=0), 1)
    step_two = norm_next / curvature
    out[:PROBES, :] = step_one * d0 + step_two * d1
    out[PROBES:, :] = r1_own - step_two * applied
    wait_send(9, small.at[3, most_r])


def solution(mesh):
    nrow, ncol = mesh.shape["row"], mesh.shape["col"]
    xs, ys = ncol // CORES, nrow // ZS
    ngc, ngr = ZS * CORES, xs * ys

    def body(points, inv_lengths, signal_level, noise_level, right_sides, block_counts):
        vmem, smem = pl.BlockSpec(memory_space=pltpu.VMEM), pl.BlockSpec(memory_space=pltpu.SMEM)
        anywhere = pl.BlockSpec(memory_space=pl.ANY)
        result = pl.pallas_call(
            functools.partial(kernel, ngc, ngr, xs),
            out_shape=jax.ShapeDtypeStruct((2 * PROBES, BLOCK), F32),
            in_specs=[smem, smem, smem, anywhere, anywhere, anywhere],
            out_specs=vmem,
            scratch_shapes=[
                pltpu.VMEM((FEAT, BLOCK), F32),
                pltpu.VMEM((1, FEAT), F32),
                pltpu.VMEM((PROBES, BLOCK), F32),
                pltpu.SemaphoreType.DMA((3,)),
                pltpu.VMEM((FEAT, BLOCK), F32),
                pltpu.VMEM((PROBES, BLOCK), F32),
                pltpu.VMEM((PROBES, BLOCK), BF16),
                pltpu.VMEM((PROBES, BLOCK), BF16),
                pltpu.VMEM((PROBES, BLOCK), F32),
                pltpu.VMEM((4, 1, 128), F32),
                pltpu.VMEM((ngc, FEAT, BLOCK), F32),
                pltpu.VMEM((ngr, FEAT, BLOCK), F32),
                pltpu.VMEM((ngc, PROBES, BLOCK), BF16),
                pltpu.VMEM((ngc, PROBES, BLOCK), F32),
                pltpu.VMEM((ngc, PROBES, BLOCK), F32),
                pltpu.VMEM((ngr, PROBES, BLOCK), BF16),
                pltpu.VMEM((2, ngr, PROBES, BLOCK), F32),
                pltpu.VMEM((2, ngr, PROBES, BLOCK), F32),
                pltpu.VMEM((4, ngc, 1, 128), F32),
                pltpu.VMEM((DEPTH, ngr * BLOCK), BF16),
                pltpu.VMEM((ngc * BLOCK, DEPTH), BF16),
                pltpu.VMEM((PROBES, ngc * BLOCK), BF16),
                pltpu.VMEM((ngc * BLOCK, ngr * BLOCK), BF16),
                pltpu.SemaphoreType.DMA((12,)),
                pltpu.SemaphoreType.DMA((12,)),
                pltpu.SemaphoreType.DMA((4,)),
                pltpu.SemaphoreType.DMA((ngc,)),
                pltpu.SemaphoreType.DMA((ngr,)),
                pltpu.SemaphoreType.DMA((ngc,)),
                pltpu.SemaphoreType.DMA((ngc,)),
                pltpu.SemaphoreType.DMA((ngc,)),
            ],
            compiler_params=pltpu.CompilerParams(
                collective_id=0, has_side_effects=True, vmem_limit_bytes=60 * 1024 * 1024
            ),
            name="cg",
        )(block_counts, signal_level, noise_level, points.T, inv_lengths.reshape(1, FEAT), right_sides.T)
        return result[:PROBES].T, result[PROBES:].T

    in_specs = (P(("row", "col"), None), P(), P(), P(), P(("row", "col"), None), P(("row", "col")))
    out_specs = (P(("row", "col"), None), P(("row", "col"), None))
    return jax.shard_map(body, mesh=mesh, in_specs=in_specs, out_specs=out_specs, check_vma=False)
```

```python
import functools

import jax
import jax.numpy as jnp
from jax import lax
from jax.experimental import pallas as pl
from jax.experimental.pallas import tpu as pltpu
from jax.sharding import PartitionSpec as P

MESH = pl.DeviceIdType.MESH
F32, BF16 = jnp.float32, jnp.bfloat16
LOG2E = 1.4426950408889634

FEAT, PROBES, BLOCK = 16, 32, 256
ZS, CORES = 8, 2
DEPTH = 128


def split3(v):
    high = v.astype(BF16).astype(F32)
    rest = v - high
    mid = rest.astype(BF16).astype(F32)
    return high, mid, rest - mid


def features(points, extra, left):
    squares = jnp.sum(points * points, axis=0, keepdims=True)
    uh, um, ul = split3(extra - 0.5 * LOG2E * squares)
    row = lax.broadcasted_iota(jnp.int32, points.shape, 0)
    base, other = (0, 3) if left else (3, 0)
    tail = jnp.where(row == base, uh, jnp.where(row == base + 1, um, jnp.where(row == base + 2, ul, 0.0)))
    tail = jnp.where((row >= other) & (row < other + 3), 1.0, tail)
    h, m, l = split3(points * LOG2E if left else points)
    parts = [h, h, m, h, l, m] if left else [h, m, h, l, h, m]
    return jnp.concatenate(parts + [tail, jnp.zeros_like(points)], axis=0)


def pack(columns):
    rest = [jnp.zeros((PROBES, 1), F32)] * (128 // PROBES - len(columns))
    column = jnp.concatenate(list(columns) + rest, axis=0)
    return jnp.broadcast_to(column, (128, 128)).T[0:1, :]


def unpack(row, count):
    column = jnp.broadcast_to(row, (128, 128)).T[:, 0:1]
    return [column[i * PROBES : (i + 1) * PROBES] for i in range(count)]


def kernel(
    ngc, ngr, xs,
    count, signal, noise, points_hbm, inv_hbm, rhs_hbm,
    out,
    points, inv, rhs, load, pts_own, r0_own, d0_own, d1_own, app_own, tiles,
    pts_c, pts_r, d0_c, r0_c, app_c, d1_r, ybuf, rs_buf, small,
    amat, bmat, dmat, kmat,
    send, recv, relay, pts_sem, left_sem, d0_sem, r0_sem, ag_sem,
):
    row, col = lax.axis_index("row"), lax.axis_index("col")
    y, z = lax.div(row, ZS), lax.rem(row, ZS)
    x, core = lax.div(col, CORES), lax.rem(col, CORES)
    gc = z * CORES + core
    gr = y * xs + x
    me = (row, col)
    partner = (row, x * CORES + 1 - core)
    pairs = ngr // 2
    half = ngc * BLOCK // 2

    def around(g, k, total):
        return lax.rem(g + k, total)

    def dev_c(g):
        return (y * ZS + lax.div(g, CORES), x * CORES + lax.rem(g, CORES))

    def dev_r(g):
        return (lax.div(g, xs) * ZS + z, lax.rem(g, xs) * CORES + core)

    def at_z(dz, c=core):
        return around(z, dz % ZS, ZS) * CORES + c

    def chip_z(dz):
        return (y * ZS + around(z, dz % ZS, ZS), col)

    def pair_at(k):
        return around(lax.div(gr, 2), k, pairs)

    peers_c = [dev_c(around(gc, k, ngc)) for k in range(1, ngc)]
    peers_r = [dev_r(2 * lax.div(gr, 2) + 1 - lax.rem(gr, 2))]
    for k in range(1, pairs):
        peers_r += [dev_r(2 * pair_at(pairs - k) + h) for h in range(2)]
    first_hops, later_hops = [1, -1, 2], [-2, 3, -3, 4]
    hops = first_hops + later_hops
    places = [(dz, side) for dz in [0] + hops for side in range(2)]
    order = [at_z(-dz, 1 - core if side else core) for dz, side in places]
    others = order[1::2]

    def copy(src, dst, ss, rs, dev):
        return pltpu.make_async_remote_copy(
            src_ref=src, dst_ref=dst, send_sem=ss, recv_sem=rs, device_id=dev, device_id_type=MESH
        )

    def wait_recv(i, dst):
        copy(dst, dst, send.at[i], recv.at[i], me).wait_recv()

    def wait_send(i, src):
        copy(src, src, send.at[i], recv.at[0], me).wait_send()

    most_c, most_r = pl.ds(0, ngc - 1), pl.ds(0, ngr - 1)

    def spread(i, block, slots, sems, targets):
        copy(block, slots.at[gc], send.at[i], sems.at[gc], partner).start()
        for dz in targets:
            copy(block, slots.at[gc], send.at[i], sems.at[gc], chip_z(dz)).start()

    def arrived(slots, sems, g):
        copy(slots.at[g], slots.at[g], send.at[0], sems.at[g], me).wait_recv()

    def hand_on(j, slots, sems, g, dev):
        copy(slots.at[g], slots.at[g], relay.at[j], sems.at[g], dev).start()

    def pass_over(j, slots, sems, distances):
        for dz in distances:
            arrived(slots, sems, at_z(-dz))
            hand_on(j, slots, sems, at_z(-dz), partner)

    def drain(i, j, slots, sent, handed):
        copy(slots.at[pl.ds(0, sent)], slots.at[pl.ds(0, sent)], send.at[i], recv.at[0], me).wait_send()
        copy(slots.at[pl.ds(0, handed)], slots.at[pl.ds(0, handed)], relay.at[j], recv.at[0], me).wait_send()

    loads = [
        pltpu.make_async_copy(source, target, load.at[i])
        for i, (source, target) in enumerate([(points_hbm, points), (inv_hbm, inv), (rhs_hbm, rhs)])
    ]
    for one in loads:
        one.start()
    barrier = pltpu.get_barrier_semaphore()
    for peer in peers_c + peers_r:
        pl.semaphore_signal(barrier, inc=1, device_id=peer, device_id_type=MESH)

    for one in loads:
        one.wait()
    inv_row = jnp.concatenate([inv[...], jnp.zeros((1, 128 - FEAT), F32)], axis=1)
    inv_column = jnp.broadcast_to(inv_row, (128, 128)).T[:FEAT, 0:1]
    own = points[...] * inv_column
    slot = lax.broadcasted_iota(jnp.int32, (1, BLOCK), 1)
    valid = (slot < count[0]).astype(F32)
    first = valid * rhs[...]
    first_bf = first.astype(BF16)
    d0 = first_bf.astype(F32)
    pts_own[...] = own
    pts_c[gc] = own
    pts_r[gr] = own
    r0_own[...] = first
    r0_c[gc] = first
    d0_own[...] = first_bf
    d0_c[gc] = first_bf
    pl.semaphore_wait(barrier, (ngc - 1) + (ngr - 1))

    spread(1, pts_own, pts_c, pts_sem, hops)
    for peer in peers_r:
        copy(pts_own, pts_r.at[gr], send.at[0], left_sem.at[gr], peer).start()
    spread(2, d0_own, d0_c, d0_sem, hops)
    spread(3, r0_own, r0_c, r0_sem, hops)

    log_signal = jnp.log(jnp.full((1, BLOCK), signal[0], F32)) * LOG2E

    def lanes_of(g, width=1):
        return pl.ds(pl.multiple_of(g * width * BLOCK, width * BLOCK), width * BLOCK)

    def right_block(i):
        right = features(pts_c[order[i]], jnp.zeros((1, BLOCK), F32), False).T.astype(BF16)
        bmat[i * BLOCK : (i + 1) * BLOCK, :] = right

    def left_block(g):
        amat[:, lanes_of(g)] = features(pts_r[g], log_signal, True).astype(BF16)

    right_block(0)
    left_block(gr)
    pass_over(0, pts_c, pts_sem, first_hops)
    for i in range(2, ngc // 2, 2):
        right_block(i)
    for i in range(1, ngc // 2, 2):
        arrived(pts_c, pts_sem, order[i])
        right_block(i)
    pass_over(0, pts_c, pts_sem, later_hops)

    def build(start, lanes):
        exponent = jnp.dot(bmat[start : start + half, :], amat[:, lanes], preferred_element_type=F32)
        values = jnp.exp2(exponent).astype(BF16)
        kmat[start : start + half, lanes] = values
        return values

    def near_part(k, _):
        quad = around(lax.div(gr, 4), k, quads)
        for h in range(4):

            @pl.when(4 * quad + h != gr)
            def _():
                arrived(pts_r, left_sem, 4 * quad + h)
                left_block(4 * quad + h)

        build(0, lanes_of(quad, 4))
        return 0

    quads = ngr // 4
    lax.fori_loop(0, quads - 1, near_part, 0)
    pass_over(1, d0_c, d0_sem, hops)
    near_part(quads - 1, 0)
    for i in range(ngc // 2, ngc, 2):
        right_block(i)
    for i in range(ngc // 2 + 1, ngc, 2):
        arrived(pts_c, pts_sem, order[i])
        right_block(i)
    for g in others:
        arrived(d0_c, d0_sem, g)
    for i, g in enumerate(order):
        dmat[:, i * BLOCK : (i + 1) * BLOCK] = d0_c[g]

    def send_image(it, j, image):
        for h in range(2):
            owner = 2 * j + h
            ybuf[it, owner] = image[:, h * BLOCK : (h + 1) * BLOCK]

            @pl.when(owner != gr)
            def _():
                copy(ybuf.at[it, owner], rs_buf.at[it, gr], send.at[4 + it], recv.at[4 + it], dev_r(owner)).start()

    def far_image(lanes):
        image = jnp.dot(dmat[:, :half], kmat[:half, lanes], preferred_element_type=F32)
        return image + jnp.dot(dmat[:, half:], build(half, lanes), preferred_element_type=F32)

    def far_part(k, _):
        j = pair_at(k)
        send_image(0, j, far_image(lanes_of(j, 2)))
        return 0

    lax.fori_loop(1, pairs, far_part, 0)
    twin = 2 * lax.div(gr, 2) + 1 - lax.rem(gr, 2)
    ybuf[0, twin] = far_image(lanes_of(twin))
    copy(ybuf.at[0, twin], rs_buf.at[0, gr], send.at[4], recv.at[4], dev_r(twin)).start()
    pass_over(2, r0_c, r0_sem, hops)
    ybuf[0, gr] = far_image(lanes_of(gr))
    def sum_of(v):
        return jnp.sum(v, axis=1, keepdims=True)

    def own_image(it, direction):
        wait_recv(4 + it, rs_buf.at[it, most_r])
        rs_buf[it, gr] = ybuf[it, gr]
        return valid * jnp.sum(rs_buf[it], axis=0) + noise[0] * direction

    def exchange(s, message, along_c):
        i = 6 + s
        group, devices = (gc, peers_c) if along_c else (gr, peers_r)
        tiles[s] = message
        small[s, group] = message
        for device in devices:
            copy(tiles.at[s], small.at[s, group], send.at[i], recv.at[i], device).start()

    def gathered(s, along_c):
        wait_recv(6 + s, small.at[s, most_c if along_c else most_r])
        return small[s]

    def lane_roll(v, shift):
        return pltpu.roll(v, shift % 128, v.ndim - 1)

    def joined(part):
        weight, vertex, least = [lane_roll(part, -PROBES * i) for i in (1, 2, 3)]
        weights = jnp.sum(weight, axis=0)
        middle = jnp.where(weights > 0.0, jnp.sum(weight * vertex, axis=0) / weights, 0.0)
        away = vertex - middle[None]
        return jnp.sum(part, axis=0), weights, middle, jnp.sum(least + weight * away * away, axis=0)

    lane = lax.broadcasted_iota(jnp.int32, (1, 128), 1)

    def side_by_side(rows):
        result = rows[0]
        for i, one in enumerate(rows[1:], 1):
            result = jnp.where(lane >= PROBES * i, lane_roll(one, PROBES * i), result)
        return result

    applied = own_image(0, d0)
    app_own[...] = applied
    app_c[gc] = applied
    spread(11, app_own, app_c, ag_sem, hops)
    weight = sum_of(applied * applied)
    vertex = jnp.where(weight > 0.0, sum_of(first * applied) / weight, 0.0)
    off = first - vertex * applied
    exchange(0, pack([sum_of(d0 * applied), weight, vertex, sum_of(off * off)]), False)
    pass_over(3, app_c, ag_sem, first_hops)
    exchange(1, side_by_side(joined(gathered(0, False))), True)
    pass_over(3, app_c, ag_sem, later_hops)
    curvature, weight, vertex, least = joined(gathered(1, True))
    norm_now = least + weight * vertex * vertex
    step_row = norm_now / curvature
    norm_next = least + weight * (step_row - vertex) * (step_row - vertex)
    step_one, beta, norm_next = unpack(side_by_side([step_row, norm_next / norm_now, norm_next]), 3)
    for g in others:
        arrived(r0_c, r0_sem, g)
    for g in others:
        arrived(app_c, ag_sem, g)
    for i, g in enumerate(order):
        r1 = r0_c[g] - step_one * app_c[g]
        dmat[:, i * BLOCK : (i + 1) * BLOCK] = (r1 + beta * d0_c[g].astype(F32)).astype(BF16)
    r1_own = first - step_one * applied
    d1_bf = (r1_own + beta * d0).astype(BF16)
    d1 = d1_bf.astype(F32)
    d1_own[...] = d1_bf
    d1_r[gr] = d1_bf
    for peer in peers_r:
        copy(d1_own, d1_r.at[gr], send.at[10], recv.at[10], peer).start()

    def second_part(k, _):
        j = pair_at(k)
        send_image(1, j, jnp.dot(dmat[...], kmat[:, lanes_of(j, 2)], preferred_element_type=F32))
        return 0

    lax.fori_loop(1, pairs + 1, second_part, 0)
    wait_recv(10, d1_r.at[most_r])
    acc = jnp.zeros((PROBES, BLOCK), F32)
    for g in range(ngr):
        acc = acc + d1_r[g].astype(F32) * ybuf[1, g]
    exchange(2, pack([sum_of(acc) + noise[0] * sum_of(d1 * d1)]), True)
    drain(1, 0, pts_c, ZS, ZS - 1)
    drain(2, 1, d0_c, ZS, ZS - 1)
    drain(3, 2, r0_c, ZS, ZS - 1)
    drain(11, 3, app_c, ZS, ZS - 1)
    wait_send(0, pts_r.at[most_r])
    wait_send(4, rs_buf.at[0, most_r])
    wait_send(6, small.at[0, most_r])
    wait_send(7, small.at[1, most_c])
    exchange(3, jnp.sum(gathered(2, True), axis=0), False)
    wait_send(8, small.at[2, most_c])
    wait_send(10, d1_r.at[most_r])
    applied = own_image(1, d1)
    wait_send(5, rs_buf.at[1, most_r])
    (curvature,) = unpack(jnp.sum(gathered(3, False), axis=0), 1)
    step_two = norm_next / curvature
    out[:PROBES, :] = step_one * d0 + step_two * d1
    out[PROBES:, :] = r1_own - step_two * applied
    wait_send(9, small.at[3, most_r])


def solution(mesh):
    nrow, ncol = mesh.shape["row"], mesh.shape["col"]
    xs, ys = ncol // CORES, nrow // ZS
    ngc, ngr = ZS * CORES, xs * ys

    def body(points, inv_lengths, signal_level, noise_level, right_sides, block_counts):
        vmem, smem = pl.BlockSpec(memory_space=pltpu.VMEM), pl.BlockSpec(memory_space=pltpu.SMEM)
        anywhere = pl.BlockSpec(memory_space=pl.ANY)
        result = pl.pallas_call(
            functools.partial(kernel, ngc, ngr, xs),
            out_shape=jax.ShapeDtypeStruct((2 * PROBES, BLOCK), F32),
            in_specs=[smem, smem, smem, anywhere, anywhere, anywhere],
            out_specs=vmem,
            scratch_shapes=[
                pltpu.VMEM((FEAT, BLOCK), F32),
                pltpu.VMEM((1, FEAT), F32),
                pltpu.VMEM((PROBES, BLOCK), F32),
                pltpu.SemaphoreType.DMA((3,)),
                pltpu.VMEM((FEAT, BLOCK), F32),
                pltpu.VMEM((PROBES, BLOCK), F32),
                pltpu.VMEM((PROBES, BLOCK), BF16),
                pltpu.VMEM((PROBES, BLOCK), BF16),
                pltpu.VMEM((PROBES, BLOCK), F32),
                pltpu.VMEM((4, 1, 128), F32),
                pltpu.VMEM((ngc, FEAT, BLOCK), F32),
                pltpu.VMEM((ngr, FEAT, BLOCK), F32),
                pltpu.VMEM((ngc, PROBES, BLOCK), BF16),
                pltpu.VMEM((ngc, PROBES, BLOCK), F32),
                pltpu.VMEM((ngc, PROBES, BLOCK), F32),
                pltpu.VMEM((ngr, PROBES, BLOCK), BF16),
                pltpu.VMEM((2, ngr, PROBES, BLOCK), F32),
                pltpu.VMEM((2, ngr, PROBES, BLOCK), F32),
                pltpu.VMEM((4, ngc, 1, 128), F32),
                pltpu.VMEM((DEPTH, ngr * BLOCK), BF16),
                pltpu.VMEM((ngc * BLOCK, DEPTH), BF16),
                pltpu.VMEM((PROBES, ngc * BLOCK), BF16),
                pltpu.VMEM((ngc * BLOCK, ngr * BLOCK), BF16),
                pltpu.SemaphoreType.DMA((12,)),
                pltpu.SemaphoreType.DMA((12,)),
                pltpu.SemaphoreType.DMA((4,)),
                pltpu.SemaphoreType.DMA((ngc,)),
                pltpu.SemaphoreType.DMA((ngr,)),
                pltpu.SemaphoreType.DMA((ngc,)),
                pltpu.SemaphoreType.DMA((ngc,)),
                pltpu.SemaphoreType.DMA((ngc,)),
            ],
            compiler_params=pltpu.CompilerParams(
                collective_id=0, has_side_effects=True, vmem_limit_bytes=60 * 1024 * 1024
            ),
            name="cg",
        )(block_counts, signal_level, noise_level, points.T, inv_lengths.reshape(1, FEAT), right_sides.T)
        return result[:PROBES].T, result[PROBES:].T

    in_specs = (P(("row", "col"), None), P(), P(), P(), P(("row", "col"), None), P(("row", "col")))
    out_specs = (P(("row", "col"), None), P(("row", "col"), None))
    return jax.shard_map(body, mesh=mesh, in_specs=in_specs, out_specs=out_specs, check_vma=False)
```

```python
import functools

import jax
import jax.numpy as jnp
from jax import lax
from jax.experimental import pallas as pl
from jax.experimental.pallas import tpu as pltpu
from jax.sharding import PartitionSpec as P

MESH = pl.DeviceIdType.MESH
F32, BF16 = jnp.float32, jnp.bfloat16
LOG2E = 1.4426950408889634

FEAT, PROBES, BLOCK = 16, 32, 256
ZS, CORES = 8, 2
DEPTH = 128


def split3(v):
    high = v.astype(BF16).astype(F32)
    rest = v - high
    mid = rest.astype(BF16).astype(F32)
    return high, mid, rest - mid


def features(points, extra, left):
    squares = jnp.sum(points * points, axis=0, keepdims=True)
    uh, um, ul = split3(extra - 0.5 * LOG2E * squares)
    row = lax.broadcasted_iota(jnp.int32, points.shape, 0)
    base, other = (0, 3) if left else (3, 0)
    tail = jnp.where(row == base, uh, jnp.where(row == base + 1, um, jnp.where(row == base + 2, ul, 0.0)))
    tail = jnp.where((row >= other) & (row < other + 3), 1.0, tail)
    h, m, l = split3(points * LOG2E if left else points)
    parts = [h, h, m, h, l, m] if left else [h, m, h, l, h, m]
    return jnp.concatenate(parts + [tail, jnp.zeros_like(points)], axis=0)


def pack(columns):
    rest = [jnp.zeros((PROBES, 1), F32)] * (128 // PROBES - len(columns))
    column = jnp.concatenate(list(columns) + rest, axis=0)
    return jnp.broadcast_to(column, (128, 128)).T[0:1, :]


def unpack(row, count):
    column = jnp.broadcast_to(row, (128, 128)).T[:, 0:1]
    return [column[i * PROBES : (i + 1) * PROBES] for i in range(count)]


def kernel(
    ngc, ngr, xs,
    count, signal, noise, points_hbm, inv_hbm, rhs_hbm,
    out,
    points, inv, rhs, load, pts_own, r0_own, d0_own, d1_own, app_own, tiles,
    pts_c, pts_r, d0_c, r0_c, app_c, d1_r, ybuf, rs_buf, small,
    amat, bmat, dmat, kmat,
    send, recv, relay, pts_sem, left_sem, d0_sem, r0_sem, ag_sem,
):
    row, col = lax.axis_index("row"), lax.axis_index("col")
    y, z = lax.div(row, ZS), lax.rem(row, ZS)
    x, core = lax.div(col, CORES), lax.rem(col, CORES)
    gc = z * CORES + core
    gr = y * xs + x
    me = (row, col)
    partner = (row, x * CORES + 1 - core)
    pairs = ngr // 2
    half = ngc * BLOCK // 2

    def around(g, k, total):
        return lax.rem(g + k, total)

    def dev_c(g):
        return (y * ZS + lax.div(g, CORES), x * CORES + lax.rem(g, CORES))

    def dev_r(g):
        return (lax.div(g, xs) * ZS + z, lax.rem(g, xs) * CORES + core)

    def at_z(dz, c=core):
        return around(z, dz % ZS, ZS) * CORES + c

    def chip_z(dz):
        return (y * ZS + around(z, dz % ZS, ZS), col)

    def pair_at(k):
        return around(lax.div(gr, 2), k, pairs)

    peers_c = [dev_c(around(gc, k, ngc)) for k in range(1, ngc)]
    peers_r = [dev_r(2 * lax.div(gr, 2) + 1 - lax.rem(gr, 2))]
    for k in range(1, pairs):
        peers_r += [dev_r(2 * pair_at(pairs - k) + h) for h in range(2)]
    first_hops, later_hops = [1, -1, 2], [-2, 3, -3, 4]
    hops = first_hops + later_hops
    places = [(dz, side) for dz in [0] + hops for side in range(2)]
    order = [at_z(-dz, 1 - core if side else core) for dz, side in places]
    others = order[1::2]

    def copy(src, dst, ss, rs, dev):
        return pltpu.make_async_remote_copy(
            src_ref=src, dst_ref=dst, send_sem=ss, recv_sem=rs, device_id=dev, device_id_type=MESH
        )

    def wait_recv(i, dst):
        copy(dst, dst, send.at[i], recv.at[i], me).wait_recv()

    def wait_send(i, src):
        copy(src, src, send.at[i], recv.at[0], me).wait_send()

    most_c, most_r = pl.ds(0, ngc - 1), pl.ds(0, ngr - 1)

    def spread(i, block, slots, sems, targets):
        copy(block, slots.at[gc], send.at[i], sems.at[gc], partner).start()
        for dz in targets:
            copy(block, slots.at[gc], send.at[i], sems.at[gc], chip_z(dz)).start()

    def arrived(slots, sems, g):
        copy(slots.at[g], slots.at[g], send.at[0], sems.at[g], me).wait_recv()

    def hand_on(j, slots, sems, g, dev):
        copy(slots.at[g], slots.at[g], relay.at[j], sems.at[g], dev).start()

    def pass_over(j, slots, sems, distances):
        for dz in distances:
            arrived(slots, sems, at_z(-dz))
            hand_on(j, slots, sems, at_z(-dz), partner)

    def drain(i, j, slots, sent, handed):
        copy(slots.at[pl.ds(0, sent)], slots.at[pl.ds(0, sent)], send.at[i], recv.at[0], me).wait_send()
        copy(slots.at[pl.ds(0, handed)], slots.at[pl.ds(0, handed)], relay.at[j], recv.at[0], me).wait_send()

    loads = [
        pltpu.make_async_copy(source, target, load.at[i])
        for i, (source, target) in enumerate([(points_hbm, points), (inv_hbm, inv), (rhs_hbm, rhs)])
    ]
    for one in loads:
        one.start()
    barrier = pltpu.get_barrier_semaphore()
    for peer in peers_c + peers_r:
        pl.semaphore_signal(barrier, inc=1, device_id=peer, device_id_type=MESH)

    for one in loads:
        one.wait()
    inv_row = jnp.concatenate([inv[...], jnp.zeros((1, 128 - FEAT), F32)], axis=1)
    inv_column = jnp.broadcast_to(inv_row, (128, 128)).T[:FEAT, 0:1]
    own = points[...] * inv_column
    slot = lax.broadcasted_iota(jnp.int32, (1, BLOCK), 1)
    valid = (slot < count[0]).astype(F32)
    first = valid * rhs[...]
    first_bf = first.astype(BF16)
    d0 = first_bf.astype(F32)
    pts_own[...] = own
    pts_c[gc] = own
    pts_r[gr] = own
    r0_own[...] = first
    r0_c[gc] = first
    d0_own[...] = first_bf
    d0_c[gc] = first_bf
    pl.semaphore_wait(barrier, (ngc - 1) + (ngr - 1))

    spread(1, pts_own, pts_c, pts_sem, hops)
    for peer in peers_r:
        copy(pts_own, pts_r.at[gr], send.at[0], left_sem.at[gr], peer).start()
    spread(2, d0_own, d0_c, d0_sem, hops)
    spread(3, r0_own, r0_c, r0_sem, hops)

    log_signal = jnp.log(jnp.full((1, BLOCK), signal[0], F32)) * LOG2E

    def lanes_of(g, width=1):
        return pl.ds(pl.multiple_of(g * width * BLOCK, width * BLOCK), width * BLOCK)

    def right_block(i):
        right = features(pts_c[order[i]], jnp.zeros((1, BLOCK), F32), False).T.astype(BF16)
        bmat[i * BLOCK : (i + 1) * BLOCK, :] = right

    def left_block(g):
        amat[:, lanes_of(g)] = features(pts_r[g], log_signal, True).astype(BF16)

    right_block(0)
    left_block(gr)
    pass_over(0, pts_c, pts_sem, first_hops)
    for i in range(2, ngc // 2, 2):
        right_block(i)
    for i in range(1, ngc // 2, 2):
        arrived(pts_c, pts_sem, order[i])
        right_block(i)
    pass_over(0, pts_c, pts_sem, later_hops)

    def build(start, lanes):
        exponent = jnp.dot(bmat[start : start + half, :], amat[:, lanes], preferred_element_type=F32)
        values = jnp.exp2(exponent).astype(BF16)
        kmat[start : start + half, lanes] = values
        return values

    def near_part(k, _):
        quad = around(lax.div(gr, 4), k, quads)
        for h in range(4):

            @pl.when(4 * quad + h != gr)
            def _():
                arrived(pts_r, left_sem, 4 * quad + h)
                left_block(4 * quad + h)

        build(0, lanes_of(quad, 4))
        return 0

    quads = ngr // 4
    lax.fori_loop(0, quads - 1, near_part, 0)
    pass_over(1, d0_c, d0_sem, hops)
    near_part(quads - 1, 0)
    for i in range(ngc // 2, ngc, 2):
        right_block(i)
    for i in range(ngc // 2 + 1, ngc, 2):
        arrived(pts_c, pts_sem, order[i])
        right_block(i)
    for g in others:
        arrived(d0_c, d0_sem, g)
    for i, g in enumerate(order):
        dmat[:, i * BLOCK : (i + 1) * BLOCK] = d0_c[g]

    def send_image(it, j, image):
        for h in range(2):
            owner = 2 * j + h
            ybuf[it, owner] = image[:, h * BLOCK : (h + 1) * BLOCK]

            @pl.when(owner != gr)
            def _():
                copy(ybuf.at[it, owner], rs_buf.at[it, gr], send.at[4 + it], recv.at[4 + it], dev_r(owner)).start()

    def far_image(lanes):
        image = jnp.dot(dmat[:, :half], kmat[:half, lanes], preferred_element_type=F32)
        return image + jnp.dot(dmat[:, half:], build(half, lanes), preferred_element_type=F32)

    def far_part(k, _):
        j = pair_at(k)
        send_image(0, j, far_image(lanes_of(j, 2)))
        return 0

    lax.fori_loop(1, pairs, far_part, 0)
    twin = 2 * lax.div(gr, 2) + 1 - lax.rem(gr, 2)
    ybuf[0, twin] = far_image(lanes_of(twin))
    copy(ybuf.at[0, twin], rs_buf.at[0, gr], send.at[4], recv.at[4], dev_r(twin)).start()
    pass_over(2, r0_c, r0_sem, hops)
    ybuf[0, gr] = far_image(lanes_of(gr))
    def sum_of(v):
        return jnp.sum(v, axis=1, keepdims=True)

    def own_image(it, direction):
        wait_recv(4 + it, rs_buf.at[it, most_r])
        rs_buf[it, gr] = ybuf[it, gr]
        return valid * jnp.sum(rs_buf[it], axis=0) + noise[0] * direction

    def exchange(s, message, along_c):
        i = 6 + s
        group, devices = (gc, peers_c) if along_c else (gr, peers_r)
        tiles[s] = message
        small[s, group] = message
        for device in devices:
            copy(tiles.at[s], small.at[s, group], send.at[i], recv.at[i], device).start()

    def gathered(s, along_c):
        wait_recv(6 + s, small.at[s, most_c if along_c else most_r])
        return small[s]

    def lane_roll(v, shift):
        return pltpu.roll(v, shift % 128, v.ndim - 1)

    def joined(part):
        weight, vertex, least = [lane_roll(part, -PROBES * i) for i in (1, 2, 3)]
        weights = jnp.sum(weight, axis=0)
        middle = jnp.where(weights > 0.0, jnp.sum(weight * vertex, axis=0) / weights, 0.0)
        away = vertex - middle[None]
        return jnp.sum(part, axis=0), weights, middle, jnp.sum(least + weight * away * away, axis=0)

    lane = lax.broadcasted_iota(jnp.int32, (1, 128), 1)

    def side_by_side(rows):
        result = rows[0]
        for i, one in enumerate(rows[1:], 1):
            result = jnp.where(lane >= PROBES * i, lane_roll(one, PROBES * i), result)
        return result

    applied = own_image(0, d0)
    app_own[...] = applied
    app_c[gc] = applied
    spread(11, app_own, app_c, ag_sem, (4, 3, -3, 2, -2, 1, -1))
    weight = sum_of(applied * applied)
    vertex = jnp.where(weight > 0.0, sum_of(first * applied) / weight, 0.0)
    off = first - vertex * applied
    exchange(0, pack([sum_of(d0 * applied), weight, vertex, sum_of(off * off)]), False)
    exchange(1, side_by_side(joined(gathered(0, False))), True)
    pass_over(3, app_c, ag_sem, (4, 3, -3, 2, -2, 1, -1))
    curvature, weight, vertex, least = joined(gathered(1, True))
    norm_now = least + weight * vertex * vertex
    step_row = norm_now / curvature
    norm_next = least + weight * (step_row - vertex) * (step_row - vertex)
    step_one, beta, norm_next = unpack(side_by_side([step_row, norm_next / norm_now, norm_next]), 3)
    for g in others:
        arrived(r0_c, r0_sem, g)
    for g in others:
        arrived(app_c, ag_sem, g)
    for i, g in enumerate(order):
        r1 = r0_c[g] - step_one * app_c[g]
        dmat[:, i * BLOCK : (i + 1) * BLOCK] = (r1 + beta * d0_c[g].astype(F32)).astype(BF16)
    r1_own = first - step_one * applied
    d1_bf = (r1_own + beta * d0).astype(BF16)
    d1 = d1_bf.astype(F32)
    d1_own[...] = d1_bf
    d1_r[gr] = d1_bf
    for peer in peers_r:
        copy(d1_own, d1_r.at[gr], send.at[10], recv.at[10], peer).start()

    def second_part(k, _):
        j = pair_at(k)
        send_image(1, j, jnp.dot(dmat[...], kmat[:, lanes_of(j, 2)], preferred_element_type=F32))
        return 0

    lax.fori_loop(1, pairs + 1, second_part, 0)
    wait_recv(10, d1_r.at[most_r])
    acc = jnp.zeros((PROBES, BLOCK), F32)
    for g in range(ngr):
        acc = acc + d1_r[g].astype(F32) * ybuf[1, g]
    exchange(2, pack([sum_of(acc) + noise[0] * sum_of(d1 * d1)]), True)
    drain(1, 0, pts_c, ZS, ZS - 1)
    drain(2, 1, d0_c, ZS, ZS - 1)
    drain(3, 2, r0_c, ZS, ZS - 1)
    drain(11, 3, app_c, ZS, ZS - 1)
    wait_send(0, pts_r.at[most_r])
    wait_send(4, rs_buf.at[0, most_r])
    wait_send(6, small.at[0, most_r])
    wait_send(7, small.at[1, most_c])
    exchange(3, jnp.sum(gathered(2, True), axis=0), False)
    wait_send(8, small.at[2, most_c])
    wait_send(10, d1_r.at[most_r])
    applied = own_image(1, d1)
    wait_send(5, rs_buf.at[1, most_r])
    (curvature,) = unpack(jnp.sum(gathered(3, False), axis=0), 1)
    step_two = norm_next / curvature
    out[:PROBES, :] = step_one * d0 + step_two * d1
    out[PROBES:, :] = r1_own - step_two * applied
    wait_send(9, small.at[3, most_r])


def solution(mesh):
    nrow, ncol = mesh.shape["row"], mesh.shape["col"]
    xs, ys = ncol // CORES, nrow // ZS
    ngc, ngr = ZS * CORES, xs * ys

    def body(points, inv_lengths, signal_level, noise_level, right_sides, block_counts):
        vmem, smem = pl.BlockSpec(memory_space=pltpu.VMEM), pl.BlockSpec(memory_space=pltpu.SMEM)
        anywhere = pl.BlockSpec(memory_space=pl.ANY)
        result = pl.pallas_call(
            functools.partial(kernel, ngc, ngr, xs),
            out_shape=jax.ShapeDtypeStruct((2 * PROBES, BLOCK), F32),
            in_specs=[smem, smem, smem, anywhere, anywhere, anywhere],
            out_specs=vmem,
            scratch_shapes=[
                pltpu.VMEM((FEAT, BLOCK), F32),
                pltpu.VMEM((1, FEAT), F32),
                pltpu.VMEM((PROBES, BLOCK), F32),
                pltpu.SemaphoreType.DMA((3,)),
                pltpu.VMEM((FEAT, BLOCK), F32),
                pltpu.VMEM((PROBES, BLOCK), F32),
                pltpu.VMEM((PROBES, BLOCK), BF16),
                pltpu.VMEM((PROBES, BLOCK), BF16),
                pltpu.VMEM((PROBES, BLOCK), F32),
                pltpu.VMEM((4, 1, 128), F32),
                pltpu.VMEM((ngc, FEAT, BLOCK), F32),
                pltpu.VMEM((ngr, FEAT, BLOCK), F32),
                pltpu.VMEM((ngc, PROBES, BLOCK), BF16),
                pltpu.VMEM((ngc, PROBES, BLOCK), F32),
                pltpu.VMEM((ngc, PROBES, BLOCK), F32),
                pltpu.VMEM((ngr, PROBES, BLOCK), BF16),
                pltpu.VMEM((2, ngr, PROBES, BLOCK), F32),
                pltpu.VMEM((2, ngr, PROBES, BLOCK), F32),
                pltpu.VMEM((4, ngc, 1, 128), F32),
                pltpu.VMEM((DEPTH, ngr * BLOCK), BF16),
                pltpu.VMEM((ngc * BLOCK, DEPTH), BF16),
                pltpu.VMEM((PROBES, ngc * BLOCK), BF16),
                pltpu.VMEM((ngc * BLOCK, ngr * BLOCK), BF16),
                pltpu.SemaphoreType.DMA((12,)),
                pltpu.SemaphoreType.DMA((12,)),
                pltpu.SemaphoreType.DMA((4,)),
                pltpu.SemaphoreType.DMA((ngc,)),
                pltpu.SemaphoreType.DMA((ngr,)),
                pltpu.SemaphoreType.DMA((ngc,)),
                pltpu.SemaphoreType.DMA((ngc,)),
                pltpu.SemaphoreType.DMA((ngc,)),
            ],
            compiler_params=pltpu.CompilerParams(
                collective_id=0, has_side_effects=True, vmem_limit_bytes=60 * 1024 * 1024
            ),
            name="cg",
        )(block_counts, signal_level, noise_level, points.T, inv_lengths.reshape(1, FEAT), right_sides.T)
        return result[:PROBES].T, result[PROBES:].T

    in_specs = (P(("row", "col"), None), P(), P(), P(), P(("row", "col"), None), P(("row", "col")))
    out_specs = (P(("row", "col"), None), P(("row", "col"), None))
    return jax.shard_map(body, mesh=mesh, in_specs=in_specs, out_specs=out_specs, check_vma=False)
```
